32 devices in a mesh: row: 8 (over z, y), col: 4 (over x, core).
Axes of the slice: x: 2, y: 2, z: 4, core: 2. Of those that a mesh axis runs over, the one named last changes fastest.
Arguments:
- tokens: bfloat16 [16384, 1280], P('row', 'col'), may hold values from -6 to 6
- query_weight: bfloat16 [1280, 1280], P('row', 'col'), may hold values from -0.25 to 0.25
- key_weight: bfloat16 [1280, 1280], P('row', 'col'), may hold values from -0.25 to 0.25
- value_weight: bfloat16 [1280, 1280], P('row', 'col'), may hold values from -0.15625 to 0.15625
- out_weight: bfloat16 [1280, 1280], P('col', 'row'), may hold values from -1.25 to 1.25
- up_weight: bfloat16 [1280, 1280], P('row', 'col'), may hold values from -0.15625 to 0.15625
- down_weight: bfloat16 [1280, 1280], P('col', 'row'), may hold values from -0.15625 to 0.15625
- query_bias: float32 [1280], P('col'), may hold values from -3 to 3
- value_bias: float32 [1280], P('col'), may hold values from -3 to 3
- out_bias: float32 [1280], P('col'), may hold values from -3 to 3
- up_bias: float32 [1280], P('col'), may hold values from -3 to 3
- down_bias: float32 [1280], P('col'), may hold values from -3 to 3
- first_gain: float32 [1280], P('col'), may hold values from 0.5 to 1.5
- first_shift: float32 [1280], P('col'), may hold values from -3 to 3
- second_gain: float32 [1280], P('col'), may hold values from 0.5 to 1.5
- second_shift: float32 [1280], P('col'), may hold values from -3 to 3
- continuation_lengths: int32 [8, 8], P('row'), may hold values from 32 to 128, as said below
- cotangent: bfloat16 [16384, 1280], P('row', 'col'), may hold values from -6 to 6
Outputs:
- block_out: bfloat16 [16384, 1280], P('row', 'col')
- output_scale: float32 [16384], P('row')
- tokens_grad: float32 [16384, 1280], P('row', 'col')
- query_grad: float32 [1280, 1280], P('row', 'col')
- key_grad: float32 [1280, 1280], P('row', 'col')
- value_grad: float32 [1280, 1280], P('row', 'col')
- out_grad: float32 [1280, 1280], P('col', 'row')
- up_grad: float32 [1280, 1280], P('row', 'col')
- down_grad: float32 [1280, 1280], P('col', 'row')
- querybias_grad: float32 [1280], P('col')
- valuebias_grad: float32 [1280], P('col')
- outbias_grad: float32 [1280], P('col')
- upbias_grad: float32 [1280], P('col')
- downbias_grad: float32 [1280], P('col')
- firstgain_grad: float32 [1280], P('col')
- firstshift_grad: float32 [1280], P('col')
- secondgain_grad: float32 [1280], P('col')
- secondshift_grad: float32 [1280], P('col')
The draws below stay inside these ranges and needn't reach their ends.
Inputs may be any that keep to these rules, and one draw needn't show every extreme that they name: `continuation_lengths`: in every group at least one continuation uses all 128 slots.
All inputs are finite; a program needn't handle non-finite values.
Results may differ from the reference program's by a relative error of at most 0.017.
Values may be sent and summed in bfloat16 or wider, within the bound.
No kernel may reach another device: no remote copies, remote signals or barrier semaphores. Data moves between devices by JAX's collectives and lax.ppermute only.
A program may use at most 192 MiB of HBM per device.

```python
import jax
import jax.numpy as jnp
from jax import lax

D = 1280
HEAD_DIM = 160
FF = 1280
PROMPT = 1024
CONT_LEN = 128
CONTS = 8
GROUPS = 8
GROUP_TOK = 2048
TOKENS = 16384


def draw_continuation_lengths(key, part):
    draw_key, pick_key = jax.random.split(jax.random.fold_in(key, 17))
    lengths = jax.random.randint(draw_key, (GROUPS, CONTS), CONT_LEN // 4, CONT_LEN + 1)
    chosen = jax.random.randint(pick_key, (GROUPS, 1), 0, CONTS)
    column = jnp.arange(CONTS)[None, :]
    return jnp.where(column == chosen, CONT_LEN, lengths).astype(jnp.int32)


def steps_of(stream_key, shape, cuts, least, high):
    gain, own = 1.0, jax.random.fold_in(stream_key, 6)
    for dim, shards_of in cuts:
        steps = jnp.exp(jax.random.uniform(jax.random.fold_in(own, dim), (shards_of,), jnp.float32, least / len(cuts), high / len(cuts)))
        gain = gain * jnp.repeat(steps, shape[dim] // shards_of).reshape([-1 if axis == dim else 1 for axis in range(len(shape))])
    return gain


def centred(own_key, dims, spread, bound, pieces=(), kind=jnp.bfloat16):
    values = spread * jax.random.normal(own_key, dims, jnp.float32)
    if pieces:
        values = values * steps_of(own_key, dims, pieces, -0.22, 0.18)
    return jnp.clip(values, -bound, bound).astype(kind)


def setup_inputs(seed: int = 0) -> dict:
    streams_of = jax.random.split(jax.random.key(seed), 19)
    tokens = centred(streams_of[0], (TOKENS, D), 1.0, 6.0, ((0, 8), (1, 4)))
    query_weight = centred(streams_of[1], (D, D), (D // 2) ** -0.5, 0.25, ((0, 8), (1, 4)))
    key_weight = centred(streams_of[2], (D, D), (D // 2) ** -0.5, 0.25, ((0, 8), (1, 4)))
    value_weight = centred(streams_of[3], (D, D), D ** -0.5, 0.15625, ((0, 8), (1, 4)))
    out_weight = centred(streams_of[4], (D, D), (D // 64) ** -0.5, 1.25, ((0, 4), (1, 8)))
    up_weight = centred(streams_of[5], (D, FF), D ** -0.5, 0.15625, ((0, 8), (1, 4)))
    down_weight = centred(streams_of[6], (FF, D), FF ** -0.5, 0.15625, ((0, 4), (1, 8)))
    query_bias = centred(streams_of[7], (D,), 0.5, 3.0, ((0, 4),), jnp.float32)
    value_bias = centred(streams_of[8], (D,), 0.5, 3.0, ((0, 4),), jnp.float32)
    out_bias = centred(streams_of[9], (D,), 0.3, 3.0, ((0, 4),), jnp.float32)
    up_bias = centred(streams_of[10], (FF,), 0.5, 3.0, ((0, 4),), jnp.float32)
    down_bias = centred(streams_of[11], (D,), 0.3, 3.0, ((0, 4),), jnp.float32)
    first_gain = jnp.clip(1.0 + 0.1 * jax.random.normal(streams_of[12], (D,), jnp.float32), 0.5, 1.5)
    first_shift = centred(streams_of[13], (D,), 0.3, 3.0, ((0, 4),), jnp.float32)
    second_gain = jnp.clip(1.0 + 0.1 * jax.random.normal(streams_of[14], (D,), jnp.float32), 0.5, 1.5)
    second_shift = centred(streams_of[15], (D,), 0.3, 3.0, ((0, 4),), jnp.float32)
    continuation_lengths = draw_continuation_lengths(jax.random.fold_in(streams_of[18], 71), 0)
    cotangent = centred(streams_of[17], (TOKENS, D), 1.0, 6.0, ((0, 8), (1, 4)))
    return {"tokens": tokens, "query_weight": query_weight, "key_weight": key_weight, "value_weight": value_weight, "out_weight": out_weight, "up_weight": up_weight, "down_weight": down_weight, "query_bias": query_bias, "value_bias": value_bias, "out_bias": out_bias, "up_bias": up_bias, "down_bias": down_bias, "first_gain": first_gain, "first_shift": first_shift, "second_gain": second_gain, "second_shift": second_shift, "continuation_lengths": continuation_lengths, "cotangent": cotangent}


@jax.custom_vjp
def low(v):
    return lax.optimization_barrier(v.astype(jnp.bfloat16)).astype(jnp.float32)

@jax.custom_vjp
def low_back(v):
    return v

def low_keep(v):
    return (low(v), None)

def low_pass(kept, grad):
    return (grad,)

def back_keep(v):
    return (v, None)

def back_low(kept, grad):
    return (low(grad),)
low.defvjp(low_keep, low_pass)
low_back.defvjp(back_keep, back_low)
EPS = 1e-05
NEG = -1e+30
HIGH = lax.Precision.HIGHEST

def rounded(value_in):
    return low(low_back(value_in))

def matmul(left, right):
    return jnp.dot(left, right, precision=HIGH)

def layer_norm(values, gain_in, shift_in):
    row_mean = lax.optimization_barrier(jnp.mean(values, axis=-1, keepdims=True))
    row_var = lax.optimization_barrier(jnp.mean(values * values, axis=-1, keepdims=True)) - row_mean * row_mean
    return (values - row_mean) * lax.rsqrt(row_var + EPS) * gain_in + shift_in

def gelu_tanh(pre):
    return 0.5 * pre * (1.0 + jnp.tanh(0.7978845608028654 * (pre + 0.044715 * pre * pre * pre)))

def softmax_rows(scores):
    row_top = lax.optimization_barrier(jnp.max(scores, axis=-1, keepdims=True))
    expo = jnp.exp(scores - row_top)
    return expo / lax.optimization_barrier(jnp.sum(expo, axis=-1, keepdims=True))

def token_valid(lengths):
    offset = lax.broadcasted_iota(jnp.int32, (CONTS, CONT_LEN), 1)
    cont_rows = (offset < lengths[:, None]).reshape(-1)
    return jnp.concatenate([jnp.ones((PROMPT,), dtype=bool), cont_rows])

def attention(query, key, value, lengths):
    head_count = D // HEAD_DIM
    score_scale = HEAD_DIM ** (-0.5)
    q_all = query.reshape(GROUP_TOK, head_count, HEAD_DIM)
    k_all = key.reshape(GROUP_TOK, head_count, HEAD_DIM)
    v_all = value.reshape(GROUP_TOK, head_count, HEAD_DIM)
    q_prompt, k_prompt, v_prompt = (q_all[:PROMPT], k_all[:PROMPT], v_all[:PROMPT])
    q_group = q_all[PROMPT:].reshape(CONTS, CONT_LEN, head_count, HEAD_DIM)
    k_group = k_all[PROMPT:].reshape(CONTS, CONT_LEN, head_count, HEAD_DIM)
    v_group = v_all[PROMPT:].reshape(CONTS, CONT_LEN, head_count, HEAD_DIM)
    rows_at = lax.broadcasted_iota(jnp.int32, (PROMPT, PROMPT), 0)
    cols_at = lax.broadcasted_iota(jnp.int32, (PROMPT, PROMPT), 1)
    prompt_scores = low_back(jnp.einsum('qhd,khd->hqk', q_prompt, k_prompt, precision=HIGH) * score_scale)
    prompt_scores = jnp.where((cols_at <= rows_at)[None], prompt_scores, NEG)
    prompt_probs = low(softmax_rows(prompt_scores))
    prompt_out = jnp.einsum('hqk,khd->qhd', prompt_probs, v_prompt, precision=HIGH)
    cross_scores = low_back(jnp.einsum('cqhd,khd->chqk', q_group, k_prompt, precision=HIGH) * score_scale)
    self_scores = low_back(jnp.einsum('cqhd,ckhd->chqk', q_group, k_group, precision=HIGH) * score_scale)
    q_at = lax.broadcasted_iota(jnp.int32, (CONT_LEN, CONT_LEN), 0)
    k_at = lax.broadcasted_iota(jnp.int32, (CONT_LEN, CONT_LEN), 1)
    allowed = (k_at <= q_at)[None] & (k_at[None] < lengths[:, None, None])
    self_scores = jnp.where(allowed[:, None], self_scores, NEG)
    joint = low(softmax_rows(jnp.concatenate([cross_scores, self_scores], axis=-1)))
    cross_probs = joint[..., :PROMPT]
    self_probs = joint[..., PROMPT:]
    cont_out = jnp.einsum('chqk,khd->cqhd', cross_probs, v_prompt, precision=HIGH)
    cont_out = cont_out + jnp.einsum('chqk,ckhd->cqhd', self_probs, v_group, precision=HIGH)
    return jnp.concatenate([prompt_out.reshape(PROMPT, D), cont_out.reshape(CONTS * CONT_LEN, D)], axis=0)

def forward_group(values, w_query, w_key, w_value, w_out, w_up, w_down, b_query, b_value, b_out, b_up, b_down, gain_one, shift_one, gain_two, shift_two, lengths):
    feat1 = low(layer_norm(values, gain_one, shift_one))
    query = rounded(matmul(feat1, w_query) + b_query)
    key = rounded(matmul(feat1, w_key))
    value = rounded(matmul(feat1, w_value) + b_value)
    attended = rounded(attention(query, key, value, lengths))
    branch_att = low_back(matmul(attended, w_out) + b_out)
    resid = values + branch_att
    feat2 = low(layer_norm(resid, gain_two, shift_two))
    pre = low_back(matmul(feat2, w_up) + b_up)
    hidden = low(gelu_tanh(pre))
    branch_ff = low_back(matmul(hidden, w_down) + b_down)
    return resid + branch_ff

def reference(tokens, query_weight, key_weight, value_weight, out_weight, up_weight, down_weight, query_bias, value_bias, out_bias, up_bias, down_bias, first_gain, first_shift, second_gain, second_shift, continuation_lengths, cotangent):
    params = (query_weight.astype(jnp.float32), key_weight.astype(jnp.float32), value_weight.astype(jnp.float32), out_weight.astype(jnp.float32), up_weight.astype(jnp.float32), down_weight.astype(jnp.float32), query_bias.astype(jnp.float32), value_bias.astype(jnp.float32), out_bias.astype(jnp.float32), up_bias.astype(jnp.float32), down_bias.astype(jnp.float32), first_gain.astype(jnp.float32), first_shift.astype(jnp.float32), second_gain.astype(jnp.float32), second_shift.astype(jnp.float32))
    group_tokens = tokens.astype(jnp.float32).reshape(GROUPS, GROUP_TOK, D)
    group_cot = cotangent.astype(jnp.float32).reshape(GROUPS, GROUP_TOK, D)

    def per_group(totals, items):
        values, lengths, cot_rows = items
        valid_rows = token_valid(lengths).astype(jnp.float32)

        def forward(values_in, *weights):
            return forward_group(values_in, *weights, lengths)
        outf, pullback = jax.vjp(forward, values, *params)
        grads = pullback(cot_rows * valid_rows[:, None])
        scale_rows = jnp.sqrt(lax.optimization_barrier(jnp.mean(outf * outf, axis=-1))) * valid_rows
        new_totals = tuple((total + grad for total, grad in zip(totals, grads[1:])))
        return (new_totals, (outf.astype(jnp.bfloat16), scale_rows, grads[0]))
    start = tuple((jnp.zeros(param.shape, jnp.float32) for param in params))
    totals, (outs_rows, scales, input_grads) = lax.scan(per_group, start, (group_tokens, continuation_lengths, group_cot))
    return (outs_rows.reshape(TOKENS, D), scales.reshape(TOKENS), input_grads.reshape(TOKENS, D), totals[0], totals[1], totals[2], totals[3], totals[4], totals[5], totals[6], totals[7], totals[8], totals[9], totals[10], totals[11], totals[12], totals[13], totals[14])
```

```python
import jax
import jax.numpy as jnp
from jax import lax
from jax.sharding import PartitionSpec as P

HEAD_DIM = 160
PROMPT = 1024
CONT_LEN = 128


EPS = 1e-05
NEG = -1e30


def dot_plain(left, right):
    return jnp.dot(left, right, preferred_element_type=jnp.float32)


def dot_right_t(left, right):
    return lax.dot_general(
        left, right, (((1,), (1,)), ((), ())), preferred_element_type=jnp.float32
    )


def dot_left_t(left, right):
    return lax.dot_general(
        left, right, (((0,), (0,)), ((), ())), preferred_element_type=jnp.float32
    )


def gelu_tanh(pre):
    return 0.5 * pre * (1.0 + jnp.tanh(0.7978845608028654 * (pre + 0.044715 * pre * pre * pre)))


REL = (0, 2, 1, 3)


def hop(values, axis, mask):
    size = lax.axis_size(axis)
    return lax.ppermute(values, axis, [(i, i ^ mask) for i in range(size)])


def spread_cols(values):
    near = jnp.concatenate([values, hop(values, "col", 2)], axis=-1)
    return jnp.concatenate([near, hop(near, "col", 1)], axis=-1)


def fold_cols(values):
    width = values.shape[-1] // 4
    near = values[..., : 2 * width] + hop(values[..., 2 * width :], "col", 1)
    return near[..., :width] + hop(near[..., width:], "col", 2)


def to_token_split(values, own):
    quarters = values.reshape(4, values.shape[0] // 4, values.shape[1])
    pieces = []
    for mask in REL:
        piece = lax.dynamic_index_in_dim(quarters, own ^ mask, 0, keepdims=False)
        pieces.append(hop(piece, "col", mask) if mask else piece)
    return jnp.concatenate(pieces, axis=-1)


def to_feature_split(values, own):
    width = values.shape[1] // 4
    whole = jnp.zeros((4, values.shape[0], width), values.dtype)
    for b, mask in enumerate(REL):
        piece = values[:, b * width : (b + 1) * width]
        piece = hop(piece, "col", mask) if mask else piece
        whole = lax.dynamic_update_index_in_dim(whole, piece, own ^ mask, 0)
    return whole.reshape(-1, width)


def row_phases(size):
    bits = size.bit_length() - 1
    phases = []
    at = bits
    while at > 1:
        low = max(1, at - 2)
        phases.append([m << low for m in range(1, 1 << (at - low))])
        at = low
    return phases + ([[1]] if bits else [])


def row_labels(size):
    labels = [0]
    for masks in row_phases(size):
        labels = [old ^ mask for mask in [0] + masks for old in labels]
    return labels


def row_gather(values):
    held = values[None]
    for masks in row_phases(lax.axis_size("row")):
        held = jnp.concatenate([held] + [hop(held, "row", mask) for mask in masks], axis=0)
    return held


def row_fold(values):
    held = values
    for masks in reversed(row_phases(lax.axis_size("row"))):
        count = held.shape[0] // (len(masks) + 1)
        total = held[:count].astype(jnp.float32)
        for k, mask in enumerate(masks):
            total = total + hop(held[(k + 1) * count : (k + 2) * count], "row", mask).astype(jnp.float32)
        held = total.astype(values.dtype)
    return total[0]


def piece_rows(own_row, own_col, rows):
    per_block = rows // 4
    return [(own_col ^ mask) * per_block + h for mask in REL for h in range(per_block)]


def order_in(pieces, own_row, own_col):
    size = pieces.shape[0]
    labels = row_labels(size)
    inverse = jnp.array([labels.index(e) for e in range(size)], jnp.int32)
    parts = [
        lax.dynamic_index_in_dim(pieces, inverse[holder ^ own_row], 0, keepdims=False)
        for holder in piece_rows(own_row, own_col, size)
    ]
    return jnp.concatenate(parts, axis=0)


def order_out(values, own_row, own_col):
    size = lax.axis_size("row")
    per_block = size // 4
    blocks = values.reshape(size, values.shape[0] // size, values.shape[1])
    place = jnp.array(REL, jnp.int32)
    parts = []
    for label in row_labels(size):
        target = own_row ^ label
        at = place[(target // per_block) ^ own_col] * per_block + target % per_block
        parts.append(lax.dynamic_index_in_dim(blocks, at, 0, keepdims=True))
    return jnp.concatenate(parts, axis=0)


def gather_whole(shard, own_row, own_col):
    near = jnp.concatenate([shard, hop(shard, "col", 2)], axis=1)
    half = order_in(row_gather(near), own_row, own_col)
    other = hop(half, "col", 1)
    middle = other.shape[0] // 2
    other = jnp.concatenate([other[middle:], other[:middle]], axis=0)
    return jnp.concatenate([half, other], axis=1)


def fold_whole(term, own_row, own_col):
    half = term.shape[1] // 2
    middle = term.shape[0] // 2
    other = hop(term[:, half:].astype(jnp.bfloat16), "col", 1).astype(jnp.float32)
    other = jnp.concatenate([other[middle:], other[:middle]], axis=0)
    near = (term[:, :half] + other).astype(jnp.bfloat16)
    mine = row_fold(order_out(near, own_row, own_col))
    quarter = half // 2
    far = hop(mine[:, quarter:].astype(jnp.bfloat16), "col", 2)
    return mine[:, :quarter] + far.astype(jnp.float32)


def mean_of(values, full_width):
    return jnp.sum(values, axis=1, keepdims=True) / full_width


def norm_rows(values, full_width):
    row_mean = mean_of(values, full_width)
    row_var = mean_of(values * values, full_width) - row_mean * row_mean
    inv_std = lax.rsqrt(row_var + EPS)
    return (values - row_mean) * inv_std, row_mean, inv_std


def build_masks(lengths):
    conts = lengths.shape[0]
    offset = lax.broadcasted_iota(jnp.int32, (conts, CONT_LEN), 1)
    valid_rows = jnp.concatenate(
        [jnp.ones((PROMPT,), dtype=bool), (offset < lengths[:, None]).reshape(-1)]
    )
    rows_at = lax.broadcasted_iota(jnp.int32, (PROMPT, PROMPT), 0)
    cols_at = lax.broadcasted_iota(jnp.int32, (PROMPT, PROMPT), 1)
    q_at = lax.broadcasted_iota(jnp.int32, (CONT_LEN, CONT_LEN), 0)
    k_at = lax.broadcasted_iota(jnp.int32, (CONT_LEN, CONT_LEN), 1)
    self_mask = (k_at <= q_at)[None] & (k_at[None] < lengths[:, None, None])
    return (valid_rows, cols_at <= rows_at, self_mask)


def split_heads(values, head_count, conts):
    whole = values.reshape(values.shape[0], head_count, HEAD_DIM)
    return (
        whole[:PROMPT],
        whole[PROMPT:],
        whole[PROMPT:].reshape(conts, CONT_LEN, head_count, HEAD_DIM),
    )


def to_rows(values):
    return values.transpose(1, 0, 2).reshape(values.shape[1], -1)


def to_groups(values, conts):
    return values.reshape(values.shape[0], conts, CONT_LEN).transpose(1, 0, 2)


def score_blocks(query, key, prompt_mask, self_mask, head_count, conts):
    score_scale = HEAD_DIM ** (-0.5)
    q_prompt, q_cont, q_group = split_heads(query, head_count, conts)
    k_prompt, k_cont, k_group = split_heads(key, head_count, conts)
    prompt_scores = (
        jnp.einsum("qhd,khd->hqk", q_prompt, k_prompt, preferred_element_type=jnp.float32)
        * score_scale
    )
    prompt_scores = jnp.where(prompt_mask[None], prompt_scores, NEG)
    cross_scores = (
        jnp.einsum("qhd,khd->hqk", q_cont, k_prompt, preferred_element_type=jnp.float32)
        * score_scale
    )
    self_scores = (
        jnp.einsum("cqhd,ckhd->chqk", q_group, k_group, preferred_element_type=jnp.float32)
        * score_scale
    )
    self_scores = jnp.where(self_mask[:, None], self_scores, NEG)
    return (prompt_scores, cross_scores, self_scores)


def attend(query, key, value, prompt_mask, self_mask):
    head_count = query.shape[1] // HEAD_DIM
    conts = self_mask.shape[0]
    prompt_scores, cross_scores, self_scores = score_blocks(
        query, key, prompt_mask, self_mask, head_count, conts
    )
    prompt_top = jnp.max(prompt_scores, axis=-1)
    prompt_lse = prompt_top + jnp.log(
        jnp.sum(jnp.exp(prompt_scores - prompt_top[..., None]), axis=-1)
    )
    row_top = jnp.maximum(jnp.max(cross_scores, axis=-1), to_rows(jnp.max(self_scores, axis=-1)))
    row_total = jnp.sum(jnp.exp(cross_scores - row_top[..., None]), axis=-1)
    row_total = row_total + to_rows(
        jnp.sum(jnp.exp(self_scores - to_groups(row_top, conts)[..., None]), axis=-1)
    )
    cont_lse = row_top + jnp.log(row_total)
    v_prompt, v_cont, v_group = split_heads(value, head_count, conts)
    prompt_probs = jnp.exp(prompt_scores - prompt_lse[..., None]).astype(jnp.bfloat16)
    prompt_out = jnp.einsum(
        "hqk,khd->qhd", prompt_probs, v_prompt, preferred_element_type=jnp.float32
    )
    cross_probs = jnp.exp(cross_scores - cont_lse[..., None]).astype(jnp.bfloat16)
    self_probs = jnp.exp(self_scores - to_groups(cont_lse, conts)[..., None]).astype(jnp.bfloat16)
    cont_out = jnp.einsum("hqk,khd->qhd", cross_probs, v_prompt, preferred_element_type=jnp.float32)
    cont_out = cont_out + jnp.einsum(
        "chqk,ckhd->cqhd", self_probs, v_group, preferred_element_type=jnp.float32
    ).reshape(-1, head_count, HEAD_DIM)
    attended = jnp.concatenate([prompt_out, cont_out], axis=0).reshape(query.shape[0], -1)
    return (attended, prompt_lse, cont_lse)


def attend_back(query, key, value, grad_attended, prompt_lse, cont_lse, prompt_mask, self_mask):
    head_count = query.shape[1] // HEAD_DIM
    conts = self_mask.shape[0]
    score_scale = HEAD_DIM ** (-0.5)
    tokens_here = query.shape[0]
    prompt_scores, cross_scores, self_scores = score_blocks(
        query, key, prompt_mask, self_mask, head_count, conts
    )
    q_prompt, q_cont, q_group = split_heads(query, head_count, conts)
    k_prompt, k_cont, k_group = split_heads(key, head_count, conts)
    v_prompt, v_cont, v_group = split_heads(value, head_count, conts)
    g_prompt, g_cont, g_group = split_heads(grad_attended, head_count, conts)
    prompt_probs = jnp.exp(prompt_scores - prompt_lse[..., None])
    prompt_dprob = jnp.einsum(
        "qhd,khd->hqk", g_prompt, v_prompt, preferred_element_type=jnp.float32
    )
    prompt_delta = jnp.sum(prompt_probs * prompt_dprob, axis=-1, keepdims=True)
    prompt_dscore = (prompt_probs * (prompt_dprob - prompt_delta)).astype(jnp.bfloat16)
    dq_prompt = (
        jnp.einsum("hqk,khd->qhd", prompt_dscore, k_prompt, preferred_element_type=jnp.float32)
        * score_scale
    )
    dk_prompt = jnp.einsum(
        "hqk,qhd->khd", prompt_dscore, q_prompt, preferred_element_type=jnp.float32
    )
    dv_prompt = jnp.einsum(
        "hqk,qhd->khd",
        prompt_probs.astype(jnp.bfloat16),
        g_prompt,
        preferred_element_type=jnp.float32,
    )
    group_lse = to_groups(cont_lse, conts)
    cross_probs = jnp.exp(cross_scores - cont_lse[..., None])
    self_probs = jnp.exp(self_scores - group_lse[..., None])
    cross_dprob = jnp.einsum("qhd,khd->hqk", g_cont, v_prompt, preferred_element_type=jnp.float32)
    self_dprob = jnp.einsum("cqhd,ckhd->chqk", g_group, v_group, preferred_element_type=jnp.float32)
    row_delta = jnp.sum(cross_probs * cross_dprob, axis=-1) + to_rows(
        jnp.sum(self_probs * self_dprob, axis=-1)
    )
    cross_dscore = (cross_probs * (cross_dprob - row_delta[..., None])).astype(jnp.bfloat16)
    self_dscore = (self_probs * (self_dprob - to_groups(row_delta, conts)[..., None])).astype(
        jnp.bfloat16
    )
    dq_cont = jnp.einsum("hqk,khd->qhd", cross_dscore, k_prompt, preferred_element_type=jnp.float32)
    dq_cont = dq_cont + jnp.einsum(
        "chqk,ckhd->cqhd", self_dscore, k_group, preferred_element_type=jnp.float32
    ).reshape(-1, head_count, HEAD_DIM)
    dq_cont = dq_cont * score_scale
    dk_prompt = (
        dk_prompt
        + jnp.einsum("hqk,qhd->khd", cross_dscore, q_cont, preferred_element_type=jnp.float32)
    ) * score_scale
    dk_cont = (
        jnp.einsum(
            "chqk,cqhd->ckhd", self_dscore, q_group, preferred_element_type=jnp.float32
        ).reshape(-1, head_count, HEAD_DIM)
        * score_scale
    )
    dv_prompt = dv_prompt + jnp.einsum(
        "hqk,qhd->khd", cross_probs.astype(jnp.bfloat16), g_cont, preferred_element_type=jnp.float32
    )
    dv_cont = jnp.einsum(
        "chqk,cqhd->ckhd",
        self_probs.astype(jnp.bfloat16),
        g_group,
        preferred_element_type=jnp.float32,
    ).reshape(-1, head_count, HEAD_DIM)
    grad_query = jnp.concatenate([dq_prompt, dq_cont], axis=0).reshape(tokens_here, -1)
    grad_key = jnp.concatenate([dk_prompt, dk_cont], axis=0).reshape(tokens_here, -1)
    grad_value = jnp.concatenate([dv_prompt, dv_cont], axis=0).reshape(tokens_here, -1)
    return (grad_query, grad_key, grad_value)


def per_device(
    tokens,
    query_weight,
    key_weight,
    value_weight,
    out_weight,
    up_weight,
    down_weight,
    query_bias,
    value_bias,
    out_bias,
    up_bias,
    down_bias,
    first_gain,
    first_shift,
    second_gain,
    second_shift,
    continuation_lengths,
    cotangent,
):
    bf16 = jnp.bfloat16
    own = lax.axis_index("col")
    own_row = lax.axis_index("row")
    width = tokens.shape[1]
    full_width = width * lax.axis_size("col")
    count = tokens.shape[0]
    quarter = count // 4
    valid_rows, prompt_mask, self_mask = build_masks(continuation_lengths[0])
    small = spread_cols(
        jnp.stack([first_gain, first_shift, second_gain, second_shift, out_bias, up_bias, down_bias])
    )
    gain1, shift1, gain2, shift2, b_out, b_up, b_down = [small[k] for k in range(7)]
    whole_tokens = spread_cols(tokens)
    w_qkv = order_in(
        row_gather(jnp.concatenate([query_weight, key_weight, value_weight], axis=1)), own_row, own
    )
    w_out_t = gather_whole(out_weight.T, own_row, own)
    w_up = gather_whole(up_weight, own_row, own)
    w_down_t = gather_whole(down_weight.T, own_row, own)
    cot_rows = to_token_split(cotangent, own)

    normed1, row_mean1, inv_std1 = norm_rows(whole_tokens.astype(jnp.float32), full_width)
    feat1 = (normed1 * gain1 + shift1).astype(bf16)
    qkv = dot_plain(feat1, w_qkv)
    query = (qkv[:, :width] + query_bias).astype(bf16)
    key = qkv[:, width : 2 * width].astype(bf16)
    value = (qkv[:, 2 * width :] + value_bias).astype(bf16)
    attended_f, prompt_lse, cont_lse = attend(query, key, value, prompt_mask, self_mask)
    attended = to_token_split(attended_f.astype(bf16), own)

    resid_in = lax.dynamic_slice_in_dim(whole_tokens, own * quarter, quarter, 0).astype(jnp.float32)
    valid_here = lax.dynamic_slice_in_dim(valid_rows, own * quarter, quarter, 0)
    resid = resid_in + (dot_right_t(attended, w_out_t) + b_out)
    normed2, row_mean2, inv_std2 = norm_rows(resid, full_width)
    feat2 = (normed2 * gain2 + shift2).astype(bf16)
    pre = dot_plain(feat2, w_up) + b_up
    hidden = gelu_tanh(pre).astype(bf16)
    outf = resid + (dot_right_t(hidden, w_down_t) + b_down)
    scale_here = jnp.sqrt(jnp.sum(outf * outf, axis=1) / full_width) * valid_here.astype(jnp.float32)
    scales = jnp.zeros((4, 1, quarter), jnp.float32)
    for mask in REL:
        piece = hop(scale_here[None], "col", mask) if mask else scale_here[None]
        scales = lax.dynamic_update_index_in_dim(scales, piece, own ^ mask, 0)
    output_scale = scales.reshape(-1)
    block_out = to_feature_split(outf.astype(bf16), own)

    grad_branch = cot_rows * valid_here.astype(bf16)[:, None]
    grad_hidden = dot_plain(grad_branch, w_down_t)
    down_term = dot_left_t(grad_branch, hidden)
    unused_value, gelu_pull = jax.vjp(gelu_tanh, pre)
    grad_pre = gelu_pull(grad_hidden)[0].astype(bf16)
    up_term = dot_left_t(feat2, grad_pre)
    grad_norm2 = dot_right_t(grad_pre, w_up)
    scaled2 = grad_norm2 * gain2
    grad_branch_f = grad_branch.astype(jnp.float32)
    grad_resid = grad_branch_f + inv_std2 * (
        scaled2 - mean_of(scaled2, full_width) - normed2 * mean_of(scaled2 * normed2, full_width)
    )
    grad_att = grad_resid.astype(bf16)
    out_term = dot_left_t(grad_att, attended)
    grad_attended = to_feature_split(dot_plain(grad_att, w_out_t).astype(bf16), own)
    out_grad = fold_whole(out_term, own_row, own).T
    up_grad = fold_whole(up_term, own_row, own)
    down_grad = fold_whole(down_term, own_row, own).T

    grad_query_f, grad_key_f, grad_value_f = attend_back(
        query, key, value, grad_attended, prompt_lse, cont_lse, prompt_mask, self_mask
    )
    grads = jnp.concatenate([grad_query_f, grad_key_f, grad_value_f], axis=1).astype(bf16)
    qkv_term = dot_left_t(feat1, grads)
    bias_term = jnp.sum(grads.astype(jnp.float32), axis=0)
    qkv_grad = row_fold(order_out(qkv_term.astype(bf16), own_row, own))
    part1 = dot_right_t(grads, w_qkv)
    scaled1 = part1 * gain1
    stats = jnp.stack([jnp.sum(scaled1, axis=1), jnp.sum(scaled1 * normed1, axis=1)])
    stats = stats + hop(stats, "col", 1)
    stats = (stats + hop(stats, "col", 2)) / full_width
    sent = scaled1 * inv_std1
    here = lax.dynamic_slice_in_dim(sent, own * quarter, quarter, 0) + grad_resid
    sent = lax.dynamic_update_slice_in_dim(sent, here, own * quarter, 0).astype(bf16)
    near = (
        sent[:, : 2 * width].astype(jnp.float32)
        + hop(sent[:, 2 * width :], "col", 1).astype(jnp.float32)
    ).astype(bf16)
    summed = near[:, :width].astype(jnp.float32) + hop(near[:, width:], "col", 2).astype(jnp.float32)
    tokens_grad = summed - inv_std1 * (stats[0][:, None] + normed1[:, :width] * stats[1][:, None])

    vectors = fold_cols(
        jnp.stack(
            [
                jnp.sum(grad_att.astype(jnp.float32), axis=0),
                jnp.sum(grad_pre.astype(jnp.float32), axis=0),
                jnp.sum(grad_branch_f, axis=0),
                jnp.sum(part1 * normed1, axis=0),
                jnp.sum(part1, axis=0),
                jnp.sum(grad_norm2 * normed2, axis=0),
                jnp.sum(grad_norm2, axis=0),
            ]
        )
    )
    vectors = jnp.concatenate(
        [jnp.stack([bias_term[:width], bias_term[2 * width :]]), vectors], axis=0
    )
    mask = 1
    while mask < lax.axis_size("row"):
        vectors = vectors + hop(vectors, "row", mask)
        mask *= 2
    return (
        block_out,
        output_scale,
        tokens_grad,
        qkv_grad[:, :width],
        qkv_grad[:, width : 2 * width],
        qkv_grad[:, 2 * width :],
        out_grad,
        up_grad,
        down_grad,
    ) + tuple(vectors[k] for k in range(9))


def solution(mesh):
    placed = (
        P("row", "col"),
        P("row", "col"),
        P("row", "col"),
        P("row", "col"),
        P("col", "row"),
        P("row", "col"),
        P("col", "row"),
        P("col"),
        P("col"),
        P("col"),
        P("col"),
        P("col"),
        P("col"),
        P("col"),
        P("col"),
        P("col"),
        P("row", None),
        P("row", "col"),
    )
    return jax.shard_map(
        per_device,
        mesh=mesh,
        in_specs=placed,
        out_specs=(
            P("row", "col"),
            P("row"),
            P("row", "col"),
            P("row", "col"),
            P("row", "col"),
            P("row", "col"),
            P("col", "row"),
            P("row", "col"),
            P("col", "row"),
            P("col"),
            P("col"),
            P("col"),
            P("col"),
            P("col"),
            P("col"),
            P("col"),
            P("col"),
            P("col"),
        ),
        check_vma=False,
    )
```

```python
import jax
import jax.numpy as jnp
from jax import lax
from jax.experimental import pallas as pl
from jax.experimental.pallas import tpu as pltpu
from jax.sharding import PartitionSpec as P


HEAD_DIM = 160
PROMPT = 1024
CONT_LEN = 128


EPS = 1e-05
NEG = -1e30


def dot_plain(left, right):
    return jnp.dot(left, right, preferred_element_type=jnp.float32)


def dot_right_t(left, right):
    return lax.dot_general(
        left, right, (((1,), (1,)), ((), ())), preferred_element_type=jnp.float32
    )


def dot_left_t(left, right):
    return lax.dot_general(
        left, right, (((0,), (0,)), ((), ())), preferred_element_type=jnp.float32
    )


REL = (0, 2, 1, 3)


def hop(values, axis, mask):
    size = lax.axis_size(axis)
    return lax.ppermute(values, axis, [(i, i ^ mask) for i in range(size)])


def spread_cols(values):
    near = jnp.concatenate([values, hop(values, "col", 2)], axis=-1)
    return jnp.concatenate([near, hop(near, "col", 1)], axis=-1)


def fold_cols(values):
    width = values.shape[-1] // 4
    near = values[..., : 2 * width] + hop(values[..., 2 * width :], "col", 1)
    return near[..., :width] + hop(near[..., width:], "col", 2)


def pack_rows(values):
    half = values.shape[0] // 2
    return jnp.concatenate([values[:half], values[half:]], axis=1)


def to_token_split(packed, own):
    pieces = []
    for mask in REL:
        piece = lax.dynamic_index_in_dim(packed, own ^ mask, 0, keepdims=False)
        pieces.append(hop(piece, "col", mask) if mask else piece)
    return pieces


def to_feature_split(pieces):
    return jnp.stack([hop(pieces[b], "col", m) if m else pieces[b] for b, m in enumerate(REL)])


def row_phases(size):
    bits = size.bit_length() - 1
    phases = []
    at = bits
    while at > 1:
        low = max(1, at - 2)
        phases.append([m << low for m in range(1, 1 << (at - low))])
        at = low
    return phases + ([[1]] if bits else [])


def row_labels(phases):
    labels = [0]
    for masks in phases:
        labels = [old ^ mask for mask in [0] + masks for old in labels]
    return labels


def row_gather(values, phases):
    held = [values]
    for masks in phases:
        moved = [(piece, mask) for mask in masks for piece in held]
        held = held + [hop(piece, "row", mask) for piece, mask in moved]
    return held


def row_fold(keep, send):
    total = keep.astype(jnp.float32) + hop(send, "row", 1).astype(jnp.float32)
    for masks in reversed(row_phases(lax.axis_size("row"))[:-1]):
        held = total.astype(keep.dtype)
        count = held.shape[0] // (len(masks) + 1)
        total = total[:count]
        for k, mask in enumerate(masks):
            piece = held[(k + 1) * count : (k + 2) * count]
            piece = hop(piece, "row", mask)
            total = total + piece.astype(jnp.float32)
    return total[0]


def piece_order(own_row, own_col, phases):
    per_block = lax.axis_size("row") // 4
    target = jnp.array(row_labels(phases), jnp.int32) ^ own_row
    place = jnp.array(REL, jnp.int32)
    return place[(target // per_block) ^ own_col] * per_block + target % per_block


def fold_whole(near, far, order):
    keep, send = combine(near, hop(far, "col", 1), order)
    mine = row_fold(keep, send)
    quarter = near.shape[1] // 2
    arrived = hop(mine[:, quarter:].astype(jnp.bfloat16), "col", 2)
    return mine[:, :quarter] + arrived.astype(jnp.float32)


TILE = 256


def pallas(body, grid, prefetch, in_specs, out_specs, out_shape, scratch, vmem=56 << 20):
    return pl.pallas_call(
        body,
        grid_spec=pltpu.PrefetchScalarGridSpec(
            num_scalar_prefetch=prefetch,
            grid=grid,
            in_specs=in_specs,
            out_specs=out_specs,
            scratch_shapes=scratch,
        ),
        out_shape=out_shape,
        compiler_params=pltpu.CompilerParams(
            dimension_semantics=("arbitrary",) * len(grid), vmem_limit_bytes=vmem
        ),
    )


def whole_block(shape):
    return pl.BlockSpec(shape, lambda *at: (0,) * len(shape))


def load_tokens(parts, x_ref, step, halves):
    width = parts[0].shape[1] // 2
    for side in range(2):

        @pl.when(step // halves == side)
        def _():
            for b, part in enumerate(parts):
                x_ref[:, b * width : (b + 1) * width] = part[
                    :, side * width : (side + 1) * width
                ].astype(jnp.float32)


def norm_project(parts, weight, gain, shift, q_bias, v_bias):
    half, packed = parts[0].shape
    count, width = 2 * half, packed // 2
    full = 4 * width
    heads = width // HEAD_DIM
    halves = half // TILE

    def body(a, b, c, d, w, gain, shift, q_bias, v_bias, feat, mean, inv, q, k, v, x_ref):
        load_tokens((a, b, c, d), x_ref, pl.program_id(0), halves)
        x = x_ref[...]
        row_mean = jnp.sum(x, axis=1, keepdims=True) / full
        row_var = jnp.sum(x * x, axis=1, keepdims=True) / full - row_mean * row_mean
        inv_std = lax.rsqrt(row_var + EPS)
        mean[...] = row_mean
        inv[...] = inv_std
        values = ((x - row_mean) * inv_std * gain[...] + shift[...]).astype(jnp.bfloat16)
        feat[...] = values
        out = dot_plain(values, w[...])
        for n, (ref, bias) in enumerate(((q, q_bias), (k, None), (v, v_bias))):
            part = out[:, n * width : (n + 1) * width]
            if bias is not None:
                part = part + bias[...]
            part = part.astype(jnp.bfloat16)
            for h in range(heads):
                ref[h] = part[:, h * HEAD_DIM : (h + 1) * HEAD_DIM]

    part_spec = pl.BlockSpec((TILE, packed), lambda i: (i % halves, 0))
    column = pl.BlockSpec((TILE, 1), lambda i: (i, 0))
    head_spec = pl.BlockSpec((heads, TILE, HEAD_DIM), lambda i: (0, i, 0))
    head_shape = jax.ShapeDtypeStruct((heads, count, HEAD_DIM), jnp.bfloat16)
    return pallas(
        body,
        (count // TILE,),
        0,
        [part_spec] * 4
        + [whole_block(weight.shape)]
        + [whole_block((1, full))] * 2
        + [whole_block((1, width))] * 2,
        [pl.BlockSpec((TILE, full), lambda i: (i, 0)), column, column] + [head_spec] * 3,
        [
            jax.ShapeDtypeStruct((count, full), jnp.bfloat16),
            jax.ShapeDtypeStruct((count, 1), jnp.float32),
            jax.ShapeDtypeStruct((count, 1), jnp.float32),
        ]
        + [head_shape] * 3,
        [pltpu.VMEM((TILE, full), jnp.float32)],
    )(*parts, weight, gain, shift, q_bias, v_bias)


def tile_kinds(step):
    prompt_tiles = PROMPT // TILE
    kinds = []
    done = 0
    while done < prompt_tiles:
        upto = min(done + 2, prompt_tiles)
        kinds.append((jnp.logical_and(step >= done, step < upto), upto * TILE, False))
        done = upto
    kinds.append((step >= prompt_tiles, PROMPT, True))
    return kinds


def masked_scores(q, k_ref, h, step, prompt_keys, has_own, lengths):
    scale = HEAD_DIM ** (-0.5)
    near = dot_right_t(q, k_ref[h, :prompt_keys, :]) * scale
    if not has_own:
        row = lax.broadcasted_iota(jnp.int32, near.shape, 0) + step * TILE
        col = lax.broadcasted_iota(jnp.int32, near.shape, 1)
        return jnp.where(col <= row, near, NEG), None
    own = dot_right_t(q, k_ref[h, pl.ds(step * TILE, TILE), :]) * scale
    row = lax.broadcasted_iota(jnp.int32, own.shape, 0)
    col = lax.broadcasted_iota(jnp.int32, own.shape, 1)
    allowed = jnp.zeros(own.shape, jnp.bool_)
    first = (step * TILE - PROMPT) // CONT_LEN
    for n in range(TILE // CONT_LEN):
        start = n * CONT_LEN
        within = jnp.logical_and(row >= start, col >= start)
        within = jnp.logical_and(within, row < start + CONT_LEN)
        within = jnp.logical_and(within, col < start + lengths[0, first + n])
        allowed = jnp.logical_or(allowed, within)
    return near, jnp.where(jnp.logical_and(allowed, col <= row), own, NEG)


def attend(query, key, value, lengths):
    heads, count, dim = query.shape
    pairs = count // (2 * TILE)
    width = heads * dim

    def body(lengths, q_ref, k_ref, v_ref, out, lse, hold):
        step = pl.program_id(0)
        h = pl.program_id(1)
        q = q_ref[h]
        for cond, keys, has_own in tile_kinds(step):

            @pl.when(cond)
            def _():
                near, own = masked_scores(q, k_ref, h, step, keys, has_own, lengths)
                top = jnp.max(near, axis=1, keepdims=True)
                if has_own:
                    top = jnp.maximum(top, jnp.max(own, axis=1, keepdims=True))
                near = jnp.exp(near - top)
                total = jnp.sum(near, axis=1, keepdims=True)
                acc = dot_plain(near.astype(jnp.bfloat16), v_ref[h, :keys, :])
                if has_own:
                    own = jnp.exp(own - top)
                    total = total + jnp.sum(own, axis=1, keepdims=True)
                    acc = acc + dot_plain(
                        own.astype(jnp.bfloat16), v_ref[h, pl.ds(step * TILE, TILE), :]
                    )
                lse[h] = top + jnp.log(total)
                hold[...] = (acc / total).astype(jnp.bfloat16)

        for side in range(2):
            for n in range(heads):

                @pl.when(jnp.logical_and(step % 2 == side, h == n))
                def _():
                    start = side * width + n * dim
                    out[0, :, start : start + dim] = hold[...]

    whole = whole_block((heads, count, dim))
    tile_spec = pl.BlockSpec((heads, TILE, dim), lambda i, h, s: (0, i, 0))
    return pallas(
        body,
        (count // TILE, heads),
        1,
        [tile_spec, whole, whole],
        [
            pl.BlockSpec((1, TILE, 2 * width), lambda i, h, s: (i // 2, 0, 0)),
            pl.BlockSpec((heads, TILE, 1), lambda i, h, s: (0, i, 0)),
        ],
        [
            jax.ShapeDtypeStruct((pairs, TILE, 2 * width), jnp.bfloat16),
            jax.ShapeDtypeStruct((heads, count, 1), jnp.float32),
        ],
        [pltpu.VMEM((TILE, dim), jnp.bfloat16)],
    )(lengths, query, key, value)


def attend_back(query, key, value, grads, places, lse, lengths):
    heads, count, dim = query.shape
    width = heads * dim
    scale = HEAD_DIM ** (-0.5)
    last = count // TILE - 1

    def body(lengths, places, q_ref, k_ref, v_ref, g_ref, lse_ref, dq, dk, dv, hold, dk_acc, dv_acc):
        step = pl.program_id(0)
        h = pl.program_id(1)

        @pl.when(step == 0)
        def _():
            dk_acc[h] = jnp.zeros((count, dim), jnp.float32)
            dv_acc[h] = jnp.zeros((count, dim), jnp.float32)

        for side in range(2):
            for n in range(heads):

                @pl.when(jnp.logical_and(step % 2 == side, h == n))
                def _():
                    start = side * width + n * dim
                    hold[...] = g_ref[0, :, start : start + dim]

        q = q_ref[h]
        grad = hold[...]
        level = lse_ref[h]
        for cond, keys, has_own in tile_kinds(step):

            @pl.when(cond)
            def _():
                near, own = masked_scores(q, k_ref, h, step, keys, has_own, lengths)
                near = jnp.exp(near - level)
                near_d = dot_right_t(grad, v_ref[h, :keys, :])
                delta = jnp.sum(near * near_d, axis=1, keepdims=True)
                if has_own:
                    rows = pl.ds(step * TILE, TILE)
                    own = jnp.exp(own - level)
                    own_d = dot_right_t(grad, v_ref[h, rows, :])
                    delta = delta + jnp.sum(own * own_d, axis=1, keepdims=True)
                dv_acc[h, :keys, :] += dot_left_t(near.astype(jnp.bfloat16), grad)
                near = (near * (near_d - delta)).astype(jnp.bfloat16)
                acc = dot_plain(near, k_ref[h, :keys, :])
                dk_acc[h, :keys, :] += dot_left_t(near, q)
                if has_own:
                    dv_acc[h, rows, :] = dot_left_t(own.astype(jnp.bfloat16), grad)
                    own = (own * (own_d - delta)).astype(jnp.bfloat16)
                    acc = acc + dot_plain(own, k_ref[h, rows, :])
                    dk_acc[h, rows, :] = dot_left_t(own, q)
                dq[h] = (acc * scale).astype(jnp.bfloat16)

        @pl.when(step == last)
        def _():
            dk[h] = (dk_acc[h] * scale).astype(jnp.bfloat16)
            dv[h] = dv_acc[h].astype(jnp.bfloat16)

    whole = whole_block((heads, count, dim))
    tile_spec = pl.BlockSpec((heads, TILE, dim), lambda i, h, s, p: (0, i, 0))
    shape = jax.ShapeDtypeStruct((heads, count, dim), jnp.bfloat16)
    return pallas(
        body,
        (count // TILE, heads),
        2,
        [
            tile_spec,
            whole,
            whole,
            pl.BlockSpec((1, TILE, 2 * width), lambda i, h, s, p: (p[i // 2], 0, 0)),
            pl.BlockSpec((heads, TILE, 1), lambda i, h, s, p: (0, i, 0)),
        ],
        [tile_spec, whole, whole],
        [shape] * 3,
        [
            pltpu.VMEM((TILE, dim), jnp.bfloat16),
            pltpu.VMEM((heads, count, dim), jnp.float32),
            pltpu.VMEM((heads, count, dim), jnp.float32),
        ],
    )(lengths, places, query, key, value, grads, lse)


def load_grads(refs, g_ref):
    heads, _, dim = refs[0].shape
    for n, ref in enumerate(refs):
        for h in range(heads):
            start = (n * heads + h) * dim
            g_ref[:, start : start + dim] = ref[h]


def norm_back(parts, grads, weight, gain, mean, inv, extra, own):
    half, packed = parts[0].shape
    count, width = 2 * half, packed // 2
    full = 4 * width
    heads, _, dim = grads[0].shape
    halves = half // TILE
    per_quarter = extra.shape[0] // TILE

    def body(own, a, b, c, d, dq, dk, dv, w, gain, mean, inv, extra, near, far, t1, t2, s1, s2, x_ref, g_ref):
        step = pl.program_id(0)
        load_tokens((a, b, c, d), x_ref, step, halves)
        load_grads((dq, dk, dv), g_ref)
        part = dot_right_t(g_ref[...], w[...])
        normed = (x_ref[...] - mean[...]) * inv[...]

        @pl.when(step == 0)
        def _():
            s1[...] = jnp.zeros_like(s1)
            s2[...] = jnp.zeros_like(s2)

        cross = part * normed
        s1[...] += jnp.sum(cross, axis=0, keepdims=True)
        s2[...] += jnp.sum(part, axis=0, keepdims=True)
        t1[...] = jnp.sum(part * gain[...], axis=1, keepdims=True)
        t2[...] = jnp.sum(cross * gain[...], axis=1, keepdims=True)
        x_ref[...] = part * gain[...] * inv[...]

        @pl.when(step // per_quarter == own[0])
        def _():
            x_ref[...] += extra[...]

        near[...] = x_ref[:, : full // 2].astype(jnp.bfloat16)
        far[...] = x_ref[:, full // 2 :].astype(jnp.bfloat16)

    part_spec = pl.BlockSpec((TILE, packed), lambda i, s: (i % halves, 0))
    head_spec = pl.BlockSpec((heads, TILE, dim), lambda i, s: (0, i, 0))
    column = pl.BlockSpec((TILE, 1), lambda i, s: (i, 0))
    side = pl.BlockSpec((TILE, full // 2), lambda i, s: (i, 0))
    return pallas(
        body,
        (count // TILE,),
        1,
        [part_spec] * 4
        + [head_spec] * 3
        + [whole_block(weight.shape), whole_block((1, full)), column, column]
        + [pl.BlockSpec((TILE, full), lambda i, s: (i % per_quarter, 0))],
        [side, side, column, column, whole_block((1, full)), whole_block((1, full))],
        [jax.ShapeDtypeStruct((count, full // 2), jnp.bfloat16)] * 2
        + [jax.ShapeDtypeStruct((count, 1), jnp.float32)] * 2
        + [jax.ShapeDtypeStruct((1, full), jnp.float32)] * 2,
        [
            pltpu.VMEM((TILE, full), jnp.float32),
            pltpu.VMEM((TILE, 3 * heads * dim), jnp.bfloat16),
        ],
    )(own, *parts, *grads, weight, gain, mean, inv, extra)


def weight_back(feat, grads, order):
    count, full = feat.shape
    heads, _, dim = grads[0].shape
    wide = 3 * heads * dim
    pieces = order.shape[0]
    each = full // pieces
    last = count // TILE - 1

    def body(order, f, dq, dk, dv, keep, send, sums, g_ref, acc):
        step = pl.program_id(0)
        load_grads((dq, dk, dv), g_ref)
        term = dot_left_t(f[...], g_ref[...])
        total = jnp.sum(g_ref[...].astype(jnp.float32), axis=0, keepdims=True)

        @pl.when(step == 0)
        def _():
            acc[...] = term
            sums[...] = total

        @pl.when(step > 0)
        def _():
            acc[...] += term
            sums[...] += total

        @pl.when(step == last)
        def _():
            for k in range(pieces):
                start = pl.multiple_of(order[k] * each, 8)
                out, at = (keep, k) if k < pieces // 2 else (send, k - pieces // 2)
                out[at] = acc[pl.ds(start, each), :].astype(jnp.bfloat16)

    head_spec = pl.BlockSpec((heads, TILE, dim), lambda i, s: (0, i, 0))
    return pallas(
        body,
        (count // TILE,),
        1,
        [pl.BlockSpec((TILE, full), lambda i, s: (i, 0))] + [head_spec] * 3,
        [whole_block((pieces // 2, each, wide))] * 2 + [whole_block((1, wide))],
        [jax.ShapeDtypeStruct((pieces // 2, each, wide), jnp.bfloat16)] * 2
        + [jax.ShapeDtypeStruct((1, wide), jnp.float32)],
        [pltpu.VMEM((TILE, wide), jnp.bfloat16), pltpu.VMEM((full, wide), jnp.float32)],
    )(order, feat, *grads)


def place_quarters(stacked, scales, places):
    quarters, half, packed = stacked.shape
    width = packed // 2

    def body(places, s_ref, r_ref, out, scale):
        out[:half, :] = s_ref[0, :, :width]
        out[half:, :] = s_ref[0, :, width:]
        scale[...] = r_ref[...]

    return pallas(
        body,
        (quarters,),
        1,
        [
            pl.BlockSpec((1, half, packed), lambda i, p: (p[i], 0, 0)),
            pl.BlockSpec((1, 1, 2 * half), lambda i, p: (p[i], 0, 0)),
        ],
        [
            pl.BlockSpec((2 * half, width), lambda i, p: (i, 0)),
            pl.BlockSpec((1, 1, 2 * half), lambda i, p: (i, 0, 0)),
        ],
        [
            jax.ShapeDtypeStruct((quarters * 2 * half, width), stacked.dtype),
            jax.ShapeDtypeStruct(scales.shape, scales.dtype),
        ],
        [],
    )(places, stacked, scales)


def assemble(pieces, order):
    rows, width = pieces[0].shape
    size = len(pieces)

    def body(order, *refs):
        out = refs[-1]
        for k in range(size):
            out[order[k]] = refs[k][...]

    whole = pallas(
        body,
        (1,),
        1,
        [whole_block((rows, width))] * size,
        whole_block((size, rows, width)),
        jax.ShapeDtypeStruct((size, rows, width), pieces[0].dtype),
        [],
    )(order, *pieces)
    return whole.reshape(size * rows, width)


def combine(near, other, order):
    size = order.shape[0]
    half = size // 2
    each = near.shape[0] // size
    width = near.shape[1]
    near = near.reshape(size, each, width)
    other = other.reshape(size, each, width)

    def body(order, a, b, c, d, keep, send):
        keep[...] = (a[...].astype(jnp.float32) + b[...].astype(jnp.float32)).astype(jnp.bfloat16)
        send[...] = (c[...].astype(jnp.float32) + d[...].astype(jnp.float32)).astype(jnp.bfloat16)

    block = (1, each, width)
    return pallas(
        body,
        (half,),
        1,
        [
            pl.BlockSpec(block, lambda k, order: (order[k], 0, 0)),
            pl.BlockSpec(block, lambda k, order: ((order[k] + half) % size, 0, 0)),
            pl.BlockSpec(block, lambda k, order: (order[k + half], 0, 0)),
            pl.BlockSpec(block, lambda k, order: ((order[k + half] + half) % size, 0, 0)),
        ],
        [pl.BlockSpec(block, lambda k, order: (k, 0, 0))] * 2,
        [jax.ShapeDtypeStruct((half, each, width), jnp.bfloat16)] * 2,
        [],
    )(order, near, other, near, other)


def feed_forward(parts, attended, cotangents, weights, small, own, lengths):
    half, packed = parts[0].shape
    width = packed // 2
    full = 4 * width
    middle = full // 2
    quarter = half // 2
    steps = quarter // TILE
    bf16 = jnp.bfloat16

    def turned(values):
        return jnp.concatenate([values[:, middle:], values[:, :middle]], axis=1)

    def body(
        own, lengths, ta, tb, tc, td, aa, ab, ac, ad, ca, cb, cc, cd,
        wo_h, wo_o, wu_h, wu_o, wd_h, wd_o, small,
        out, ga, scale, extra, att, feat, hid, gpre, gbr, gatt, sums, x_ref,
    ):
        step = pl.program_id(0)
        load_tokens((ta, tb, tc, td), x_ref, own[0] // 2, 1)
        for side in range(steps):

            @pl.when(step == side)
            def _():
                for b, (a, c) in enumerate(zip((aa, ab, ac, ad), (ca, cb, cc, cd))):
                    to = slice(b * width, (b + 1) * width)
                    at = slice(side * width, (side + 1) * width)
                    att[:, to] = a[:, at]
                    gbr[:, to] = c[:, at]

        slot = lax.broadcasted_iota(jnp.int32, (TILE, 1), 0) + own[0] * quarter + step * TILE
        valid = slot < PROMPT
        for c in range(lengths.shape[1]):
            start = PROMPT + c * CONT_LEN
            valid = jnp.logical_or(
                valid, jnp.logical_and(slot >= start, slot < start + lengths[0, c])
            )
        valid = valid.astype(jnp.float32)
        gain, shift = small[2:3, :], small[3:4, :]
        a = att[...]
        resid = x_ref[...] + (
            dot_right_t(a[:, :middle], wo_h[...])
            + turned(dot_right_t(a[:, middle:], wo_o[...]))
            + small[4:5, :]
        )
        row_mean = jnp.sum(resid, axis=1, keepdims=True) / full
        row_var = jnp.sum(resid * resid, axis=1, keepdims=True) / full - row_mean * row_mean
        inv_std = lax.rsqrt(row_var + EPS)
        normed = (resid - row_mean) * inv_std
        feat_in = (normed * gain + shift).astype(bf16)
        feat[...] = feat_in
        pre = jnp.concatenate(
            [dot_plain(feat_in, wu_h[...]), dot_plain(turned(feat_in), wu_o[...])], axis=1
        ) + small[5:6, :]
        coef = 0.7978845608028654
        tanh = jnp.tanh(coef * (pre + 0.044715 * pre * pre * pre))
        hidden = (0.5 * pre * (1.0 + tanh)).astype(bf16)
        hid[...] = hidden
        slope = 0.5 * (1.0 + tanh) + 0.5 * pre * (1.0 - tanh * tanh) * coef * (
            1.0 + 3.0 * 0.044715 * pre * pre
        )
        outf = resid + (
            dot_right_t(hidden[:, :middle], wd_h[...])
            + turned(dot_right_t(hidden[:, middle:], wd_o[...]))
            + small[6:7, :]
        )
        scale[...] = jnp.sqrt(jnp.sum(outf * outf, axis=1, keepdims=True) / full) * valid
        x_ref[...] = outf
        branch = gbr[...].astype(jnp.float32) * valid
        gbr[...] = branch.astype(bf16)
        branch_b = branch.astype(bf16)
        grad_pre = jnp.concatenate(
            [dot_plain(branch_b, wd_h[...]), dot_plain(turned(branch_b), wd_o[...])], axis=1
        )
        grad_pre = (grad_pre * slope).astype(bf16)
        gpre[...] = grad_pre
        grad_norm = dot_right_t(grad_pre[:, :middle], wu_h[...]) + turned(
            dot_right_t(grad_pre[:, middle:], wu_o[...])
        )
        scaled = grad_norm * gain
        cross = grad_norm * normed
        first = jnp.sum(scaled, axis=1, keepdims=True) / full
        second = jnp.sum(cross * gain, axis=1, keepdims=True) / full
        grad_resid = branch + inv_std * (scaled - first - normed * second)
        extra[...] = grad_resid
        grad_att = grad_resid.astype(bf16)
        gatt[...] = grad_att
        grad_out = jnp.concatenate(
            [dot_plain(grad_att, wo_h[...]), dot_plain(turned(grad_att), wo_o[...])], axis=1
        ).astype(bf16)

        @pl.when(step == 0)
        def _():
            sums[...] = jnp.zeros_like(sums)

        for n, term in enumerate(
            (grad_att.astype(jnp.float32), grad_pre.astype(jnp.float32), branch, cross, grad_norm)
        ):
            sums[n : n + 1, :] += jnp.sum(term, axis=0, keepdims=True)
        for side in range(steps):

            @pl.when(step == side)
            def _():
                for b in range(4):
                    at = slice(b * width, (b + 1) * width)
                    to = slice(side * width, (side + 1) * width)
                    out[b, :, to] = x_ref[:, at].astype(bf16)
                    ga[b, :, to] = grad_out[:, at]

    part_spec = pl.BlockSpec((TILE, packed), lambda i, own, s: ((own[0] % 2) * steps + i, 0))
    rows_spec = pl.BlockSpec((TILE, full), lambda i, own, s: (i, 0))
    once = pl.BlockSpec(weights[0].shape, lambda i, own, s: (0, 0), pipeline_mode=pl.Buffered(1))
    rows_b = jax.ShapeDtypeStruct((quarter, full), bf16)
    return pallas(
        body,
        (steps,),
        2,
        [part_spec] * 4
        + [whole_block((TILE, packed))] * 8
        + [once] * 6
        + [whole_block(small.shape)],
        [whole_block((4, TILE, packed))] * 2
        + [pl.BlockSpec((TILE, 1), lambda i, own, s: (i, 0))]
        + [rows_spec] * 7
        + [whole_block((8, full))],
        [jax.ShapeDtypeStruct((4, TILE, packed), bf16)] * 2
        + [
            jax.ShapeDtypeStruct((quarter, 1), jnp.float32),
            jax.ShapeDtypeStruct((quarter, full), jnp.float32),
        ]
        + [rows_b] * 6
        + [jax.ShapeDtypeStruct((8, full), jnp.float32)],
        [pltpu.VMEM((TILE, full), jnp.float32)],
        60 << 20,
    )(own, lengths, *parts, *attended, *cotangents, *weights, small)


def term_halves(left, right):
    middle = right.shape[1] // 2
    halves = []
    for part in (right[:, :middle], right[:, middle:]):
        halves.append(dot_left_t(left, part).astype(jnp.bfloat16))
    return halves


def per_device(
    tokens,
    query_weight,
    key_weight,
    value_weight,
    out_weight,
    up_weight,
    down_weight,
    query_bias,
    value_bias,
    out_bias,
    up_bias,
    down_bias,
    first_gain,
    first_shift,
    second_gain,
    second_shift,
    continuation_lengths,
    cotangent,
):
    bf16 = jnp.bfloat16
    own = lax.axis_index("col")
    own_row = lax.axis_index("row")
    width = tokens.shape[1]
    full_width = width * lax.axis_size("col")
    count = tokens.shape[0]
    quarter = count // 4
    place = jnp.array(REL, jnp.int32)
    places = place[jnp.arange(4, dtype=jnp.int32) ^ own]
    phases = row_phases(lax.axis_size("row"))
    turned = phases[-1:] + phases[:-1]
    order = piece_order(own_row, own, phases)
    at = own[None]

    packed = pack_rows(tokens)
    far = hop(packed, "col", 2)
    parts = (packed, far, hop(packed, "col", 1), hop(far, "col", 1))
    shard = jnp.concatenate([query_weight, key_weight, value_weight], axis=1)
    w_qkv = assemble(row_gather(shard, phases), order)
    small = spread_cols(
        jnp.stack([first_gain, first_shift, second_gain, second_shift, out_bias, up_bias, down_bias]),
    )
    weights = []
    for shard, way in ((out_weight.T, phases), (up_weight, phases), (down_weight.T, turned)):
        near = jnp.concatenate([shard, hop(shard, "col", 2)], axis=1)
        part = assemble(row_gather(near, way), piece_order(own_row, own, way))
        weights += [part, hop(part, "col", 1)]
    cot_quarters = cotangent.reshape(4, 2, quarter // 2, width)
    cot_pieces = to_token_split(
        jnp.concatenate([cot_quarters[:, 0], cot_quarters[:, 1]], axis=2), own
    )

    feat1, row_mean1, inv_std1, query, key, value = norm_project(
        parts, w_qkv, small[0:1], small[1:2], query_bias[None], value_bias[None]
    )
    attended_rows, lse = attend(query, key, value, continuation_lengths)
    (out_sent, ga_sent, scale_here, grad_resid, att_rows, feat2, hidden, grad_pre, branch, grad_att, sums) = (
        feed_forward(
            parts,
            to_token_split(attended_rows, own),
            cot_pieces,
            weights,
            small,
            at,
            continuation_lengths,
        )
    )
    grad_attended = to_feature_split(ga_sent)
    down_terms = term_halves(branch, hidden)
    up_terms = term_halves(feat2, grad_pre)
    out_terms = term_halves(grad_att, att_rows)
    down_grad = fold_whole(*down_terms, order).T
    up_grad = fold_whole(*up_terms, order)
    out_grad = fold_whole(*out_terms, order).T
    scale_here = scale_here.reshape(1, quarter)
    scale_pieces = [hop(scale_here, "col", m) if m else scale_here for m in REL]
    block_out, scales = place_quarters(to_feature_split(out_sent), jnp.stack(scale_pieces), places)
    output_scale = scales.reshape(-1)

    grads = attend_back(query, key, value, grad_attended, places, lse, continuation_lengths)
    keep, send, bias_term = weight_back(feat1, grads, order)
    qkv_grad = row_fold(keep, send)
    bias_term = bias_term[0]
    near, far_sent, total1, cross1, gain_term, shift_term = norm_back(
        parts, grads, w_qkv, small[0:1], row_mean1, inv_std1, grad_resid, at
    )
    stats = jnp.concatenate([total1.reshape(1, count), cross1.reshape(1, count)])
    stats = stats + hop(stats, "col", 1)
    stats = (stats + hop(stats, "col", 2)) / full_width
    near = near.astype(jnp.float32) + hop(far_sent, "col", 1).astype(jnp.float32)
    arrived = hop(pack_rows(near[:, width:].astype(bf16)), "col", 2)
    summed = near[:, :width] + jnp.concatenate(
        [arrived[:, :width], arrived[:, width:]], axis=0
    ).astype(jnp.float32)
    normed_own = (tokens.astype(jnp.float32) - row_mean1) * inv_std1
    tokens_grad = summed - inv_std1 * (stats[0][:, None] + normed_own * stats[1][:, None])

    vectors = fold_cols(jnp.concatenate([sums[:3], gain_term, shift_term, sums[3:5]]))
    vectors = jnp.concatenate(
        [jnp.stack([bias_term[:width], bias_term[2 * width :]]), vectors], axis=0
    )
    mask = 1
    while mask < lax.axis_size("row"):
        vectors = vectors + hop(vectors, "row", mask)
        mask *= 2
    return (
        block_out,
        output_scale,
        tokens_grad,
        qkv_grad[:, :width],
        qkv_grad[:, width : 2 * width],
        qkv_grad[:, 2 * width :],
        out_grad,
        up_grad,
        down_grad,
    ) + tuple(vectors[k] for k in range(9))


def solution(mesh):
    placed = (
        P("row", "col"),
        P("row", "col"),
        P("row", "col"),
        P("row", "col"),
        P("col", "row"),
        P("row", "col"),
        P("col", "row"),
        P("col"),
        P("col"),
        P("col"),
        P("col"),
        P("col"),
        P("col"),
        P("col"),
        P("col"),
        P("col"),
        P("row", None),
        P("row", "col"),
    )
    return jax.shard_map(
        per_device,
        mesh=mesh,
        in_specs=placed,
        out_specs=(
            P("row", "col"),
            P("row"),
            P("row", "col"),
            P("row", "col"),
            P("row", "col"),
            P("row", "col"),
            P("col", "row"),
            P("row", "col"),
            P("col", "row"),
            P("col"),
            P("col"),
            P("col"),
            P("col"),
            P("col"),
            P("col"),
            P("col"),
            P("col"),
            P("col"),
        ),
        check_vma=False,
    )
```
